128 devices in a mesh: energy: 32 (over y, x_hi, z), tile: 4 (over x_lo, core).
Axes of the slice: x: 4 (x_hi: 2, x_lo: 2; x = x_hi * 2 + x_lo), y: 4, z: 4, core: 2. Of those that a mesh axis runs over, the one named last changes fastest.
Arguments:
- gr_electron: bfloat16 [128, 2, 512, 512], P(('energy', 'tile')), may hold values from -0.1875 to 0.1875
- self_lesser: bfloat16 [128, 2, 512, 512], P(('energy', 'tile')), may hold values from -6 to 6
- self_greater: bfloat16 [128, 2, 512, 512], P(('energy', 'tile')), may hold values from -6 to 6
- gr_boson: bfloat16 [128, 2, 512, 512], P(('energy', 'tile')), may hold values from -0.1875 to 0.1875
Outputs:
- lesser_new: bfloat16 [128, 2, 512, 512], P(('energy', 'tile'))
The draws below stay inside these ranges and needn't reach their ends.
All inputs are finite; a program needn't handle non-finite values.
Results may differ from the reference program's by a relative error of at most 0.025.
Values may be sent and summed in bfloat16 or wider, within the bound.
A program may use at most 64 MiB of HBM per device.

```python
import jax
import jax.numpy as jnp
from jax import lax

N = 512
NE = 128
NB = 128


def shard_levels(own_key, shape, cuts, low, high):
    factor_of = 1.0
    for position, shards_of in cuts:
        draws = jax.random.uniform(jax.random.fold_in(jax.random.fold_in(own_key, 6), position), (shards_of,), jnp.float32, low / len(cuts), high / len(cuts))
        factor_of = factor_of * jnp.repeat(jnp.exp(draws), shape[position] // shards_of).reshape((-1,) + (1,) * (len(shape) - 1 - position))
    return factor_of


def bell_draw(key, extent, scale, most, split=(), kind=jnp.bfloat16):
    drawn = jax.random.normal(key, extent, jnp.float32) * scale
    if len(split) > 0:
        drawn = shard_levels(key, extent, split, -0.22, 0.18) * drawn
    return jnp.clip(drawn, min=-most, max=most).astype(kind)


def setup_inputs(seed: int = 0) -> dict:
    key_list = jax.random.split(jax.random.key(seed), 5)
    return {
        "gr_electron": bell_draw(key_list[0], (NE, 2, N, N), (2 * N) ** -0.5, 0.1875, ((0, 128),)),
        "self_lesser": bell_draw(key_list[1], (NE, 2, N, N), 0.7071, 6.0, ((0, 128),)),
        "self_greater": bell_draw(key_list[2], (NE, 2, N, N), 0.7071, 6.0, ((0, 128),)),
        "gr_boson": bell_draw(key_list[3], (NB, 2, N, N), (2 * N) ** -0.5, 0.1875, ((0, 128),)),
    }


def sandwich_one(outer, middle):
    outer_re = outer[0]
    outer_im = outer[1]
    middle_re = middle[0]
    middle_im = middle[1]
    left_re = (jnp.dot(outer_re, middle_re, preferred_element_type=jnp.float32) - jnp.dot(outer_im, middle_im, preferred_element_type=jnp.float32)).astype(jnp.bfloat16)
    left_im = (jnp.dot(outer_re, middle_im, preferred_element_type=jnp.float32) + jnp.dot(outer_im, middle_re, preferred_element_type=jnp.float32)).astype(jnp.bfloat16)
    right_re = jnp.dot(left_re, outer_re.T, preferred_element_type=jnp.float32) + jnp.dot(left_im, outer_im.T, preferred_element_type=jnp.float32)
    right_im = jnp.dot(left_im, outer_re.T, preferred_element_type=jnp.float32) - jnp.dot(left_re, outer_im.T, preferred_element_type=jnp.float32)
    return jnp.stack([right_re, right_im], axis=0).astype(jnp.bfloat16)


def sandwich_all(outer, middle):
    return lax.map(lambda pair: sandwich_one(pair[0], pair[1]), (outer, middle))


def reference(gr_electron, self_lesser, self_greater, gr_boson):
    lesser = sandwich_all(gr_electron, self_lesser)
    greater = sandwich_all(gr_electron, self_greater)
    length = NE + NB
    width = lesser.shape[2]
    row_block = min(32, width)
    blocks = width // row_block

    def to_blocks(field):
        return jnp.moveaxis(field.reshape(field.shape[0], 2, blocks, row_block, width), 2, 0)

    def from_blocks(field):
        return jnp.moveaxis(field, 0, 2).reshape(field.shape[1], 2, width, width)

    def spectrum(field):
        values = lax.complex(field[:, 0].astype(jnp.float32), field[:, 1].astype(jnp.float32))
        return jnp.fft.fft(values, n=length, axis=0)

    def polar_block(pair):
        spec_lesser = spectrum(pair[0])
        spec_greater = spectrum(pair[1])
        corr = jnp.fft.ifft(spec_lesser * jnp.conj(spec_greater), axis=0)[:NB] * (NE ** -0.5)
        return jnp.stack([corr.real, corr.imag], axis=1).astype(jnp.bfloat16)

    polar = from_blocks(lax.map(polar_block, (to_blocks(lesser), to_blocks(greater))))
    screened = sandwich_all(gr_boson, polar)

    def self_block(pair):
        spec_lesser = spectrum(pair[0])
        spec_screened = spectrum(pair[1])
        conv = jnp.fft.ifft(spec_lesser * spec_screened, axis=0)[:NE] * (NB ** -0.5)
        return jnp.stack([conv.real, conv.imag], axis=1).astype(jnp.bfloat16)

    self_gw = from_blocks(lax.map(self_block, (to_blocks(lesser), to_blocks(screened))))
    return sandwich_all(gr_electron, self_gw)
```

```python
import functools
import math

import jax
import jax.numpy as jnp
import numpy as np
from jax import lax
from jax.experimental import pallas as pl
from jax.experimental.pallas import tpu as pltpu
from jax.sharding import PartitionSpec as P

MESH = pl.DeviceIdType.MESH
ROWS = 16
LANES = 128
BF16 = jnp.bfloat16
F32 = jnp.float32


class Plan:
    def __init__(self, n_energy, n_tile, width):
        self.n_energy, self.n_tile, self.width = n_energy, n_tile, width
        self.devices = n_energy * n_tile
        self.ny = 4 if n_energy % 4 == 0 else 2
        self.nxh = 2 if n_energy // self.ny == 8 else 1
        self.nz = n_energy // (self.ny * self.nxh)
        self.nxl = 2 if n_tile == 4 else 1
        self.nc = n_tile // self.nxl
        self.nx = self.nxh * self.nxl
        self.row_tiles = width // ROWS
        self.col_tiles = width // LANES
        assert self.row_tiles == n_energy and self.col_tiles == n_tile
        self.half = width // 2
        self.half_tiles = self.row_tiles // 2

    def place(self):
        e = lax.axis_index("energy")
        t = lax.axis_index("tile")
        y = e // (self.nxh * self.nz)
        x = (e // self.nz) % self.nxh * self.nxl + t // self.nc
        return y, x, e % self.nz, t % self.nc

    def device(self, y, x, z, c):
        return ((y * self.nxh + x // self.nxl) * self.nz + z, x % self.nxl * self.nc + c)


def spread(plan, place, j, y_of):
    y, x, z, c = place
    n_y, find_y = y_of
    sign = 1 - 2 * c
    j_x = j // n_y % plan.nx
    j_z = j // (n_y * plan.nx) % plan.nz
    j_c = j // (n_y * plan.nx * plan.nz)
    return plan.device(
        find_y(y, sign, j % n_y),
        (x + plan.nx + sign * j_x) % plan.nx,
        (z + plan.nz + sign * j_z) % plan.nz,
        (c + j_c) % plan.nc,
    )


def everyone(plan):
    return (plan.ny, lambda y, sign, j: (y + plan.ny + sign * j) % plan.ny)


def half_y(plan, k):
    span = plan.ny // 2
    return (span, lambda y, sign, j: (y // span + 1 + k) % 2 * span + (y % span + j) % span)


def remote(src, dst, send_sem, recv_sem, who):
    pltpu.make_async_remote_copy(
        src_ref=src, dst_ref=dst, send_sem=send_sem, recv_sem=recv_sem, device_id=who, device_id_type=MESH
    ).start()


def kernel(
    plan,
    scale,
    gre_hbm,
    sl_hbm,
    sg_hbm,
    grb_hbm,
    fwd_hbm,
    inv_hbm,
    out_hbm,
    r_e,
    r_b,
    mid,
    fwd,
    inv,
    lesser_out,
    greater_out,
    screen_out,
    lesser_in,
    greater_in,
    screen_in,
    polar_out,
    polar_in,
    self_out,
    self_in,
    wide,
    spec_l,
    result,
    in_sem,
    send_sem,
    recv_sem,
    out_sem,
):
    width, half, dev = plan.width, plan.half, plan.devices
    place = plan.place()
    me = lax.axis_index("energy") * plan.n_tile + lax.axis_index("tile")
    me_e, me_t = lax.axis_index("energy"), lax.axis_index("tile")

    def load(src, dst, k):
        copy = pltpu.make_async_copy(src, dst, in_sem.at[k])
        copy.start()
        return copy

    lo, hi = pl.ds(0, width), pl.ds(width, width)

    def load_outer(src, dst, k):
        return [
            load(src.at[0, 0], dst.at[lo, lo], k),
            load(src.at[0, 1], dst.at[lo, hi], k + 1),
            load(src.at[0, 0], dst.at[hi, hi], k + 2),
        ]

    def load_middle(src, dst, k):
        return [
            load(src.at[0, 0], dst.at[lo, lo], k),
            load(src.at[0, 1], dst.at[lo, hi], k + 1),
            load(src.at[0, 0], dst.at[hi, hi], k + 2),
        ]

    loads_r = load_outer(gre_hbm, r_e, 0)
    loads_l = load_middle(sl_hbm, mid.at[0], 3)
    loads_g = load_middle(sg_hbm, mid.at[1], 6)
    loads_t = [load(fwd_hbm, fwd, 9), load(inv_hbm, inv, 10)]
    loads_b = load_outer(grb_hbm, r_b, 11)

    barrier = pltpu.get_barrier_semaphore()

    @pl.loop(1, dev)
    def _(j):
        who = spread(plan, place, j, everyone(plan))
        pl.semaphore_signal(barrier, inc=1, device_id=who, device_id_type=MESH)

    def negate(ref):
        ref[width:, :width] = -ref[:width, width:]

    def sandwich_half(outer, middle, row0):
        rows = pl.ds(pl.multiple_of(row0, half), half)
        left = jnp.dot(outer[rows, :], middle[...], preferred_element_type=F32).astype(BF16)
        return lax.dot_general(left, outer[...], (((1,), (1,)), ((), ())), preferred_element_type=F32).astype(BF16)

    def to_blocks(right, blocks, tile0):
        for part in range(2):
            for ct in range(plan.col_tiles):
                piece = right[:, part * width + ct * LANES : part * width + (ct + 1) * LANES]
                blocks[pl.ds(tile0, plan.half_tiles), ct, part * ROWS : (part + 1) * ROWS, :] = piece.reshape(
                    plan.half_tiles, ROWS, LANES
                )

    def send_half(blocks, landing, k, phase):
        n = dev // 2

        @pl.loop(k, n)
        def _(j):
            who = spread(plan, place, j, half_y(plan, k))
            remote(blocks.at[who[0], who[1]], landing.at[me], send_sem.at[phase], recv_sem.at[phase], who)

    def sandwich_and_send(outer, middle, blocks, landing, phase, before_send=None):
        span = plan.ny // 2
        for k in range(2):
            h = (place[0] // span + 1 + k) % 2
            right = sandwich_half(outer, middle, h * half)
            to_blocks(right, blocks, h * plan.half_tiles)
            if k == 0 and before_send is not None:
                before_send()
            send_half(blocks, landing, k, phase)
        landing[me] = blocks[me_e, me_t]

    def wait_in(ref, phase):
        view = ref.at[pl.ds(0, dev - 1)]
        pltpu.make_async_copy(view, view, recv_sem.at[phase]).wait()

    def widen(landing):
        step = 8

        @pl.loop(0, dev // step)
        def _(i):
            block = landing[pl.ds(i * step, step)].astype(F32)
            start = pl.multiple_of(i * step * 2 * ROWS, 8)
            wide[pl.ds(start, step * 2 * ROWS), :] = block.reshape(step * 2 * ROWS, LANES)

    def columns(row):
        parts = [wide[pl.ds(part * ROWS + row, dev, stride=2 * ROWS), :].astype(BF16) for part in range(2)]
        return jnp.concatenate(parts, axis=0)

    group = 4
    length = 2 * dev

    def spectrum(g):
        x = jnp.concatenate([columns(g * group + i) for i in range(group)], axis=1)
        return jnp.dot(fwd[...], x, preferred_element_type=F32)

    def lanes_of(g):
        return slice(g * group * LANES, (g + 1) * group * LANES)

    def product_and_back(g, conj):
        spec = spectrum(g)
        s_re, s_im = spec[:length], spec[length:]
        l_re = spec_l[:length, lanes_of(g)]
        l_im = spec_l[length:, lanes_of(g)]
        if conj:
            p_re = l_re * s_re + l_im * s_im
            p_im = l_im * s_re - l_re * s_im
        else:
            p_re = l_re * s_re - l_im * s_im
            p_im = l_re * s_im + l_im * s_re
        p = jnp.concatenate([p_re.astype(BF16), p_im.astype(BF16)], axis=0)
        return jnp.dot(inv[...], p, preferred_element_type=F32) * scale

    def element_stage(conj, out_blocks):
        backs = []
        for g in range(ROWS // group):
            back = product_and_back(g, conj)
            for i in range(group):
                row = g * group + i
                for part in range(2):
                    backs_rows = back[part * dev : (part + 1) * dev, i * LANES : (i + 1) * LANES]
                    wide[pl.ds(part * ROWS + row, dev, stride=2 * ROWS), :] = backs_rows
        step = 8

        @pl.loop(0, dev // step)
        def _(i):
            start = pl.multiple_of(i * step * 2 * ROWS, 8)
            block = wide[pl.ds(start, step * 2 * ROWS), :].astype(BF16)
            out_blocks[pl.ds(i * step, step)] = block.reshape(step, 2 * ROWS, LANES)

    def send_blocks(out_blocks, landing, phase):
        @pl.loop(1, dev)
        def _(j):
            who = spread(plan, place, j, everyone(plan))
            remote(
                out_blocks.at[who[0] * plan.n_tile + who[1]],
                landing.at[me],
                send_sem.at[phase],
                recv_sem.at[phase],
                who,
            )

        landing[me] = out_blocks[me]

    def assemble(landing, dst):
        for ct in range(plan.col_tiles):
            for part in range(2):
                pieces = []
                for rt in range(plan.row_tiles):
                    pieces.append(landing[rt * plan.n_tile + ct, part * ROWS : (part + 1) * ROWS, :])
                block = jnp.concatenate(pieces, axis=0)
                if part == 0:
                    dst[:width, ct * LANES : (ct + 1) * LANES] = block
                    dst[width:, width + ct * LANES : width + (ct + 1) * LANES] = block
                else:
                    dst[:width, width + ct * LANES : width + (ct + 1) * LANES] = block
                    dst[width:, ct * LANES : (ct + 1) * LANES] = -block

    for copy in loads_r + loads_l:
        copy.wait()
    negate(r_e)
    negate(mid.at[0])
    sandwich_and_send(
        r_e, mid.at[0], lesser_out, lesser_in, 0, before_send=lambda: pl.semaphore_wait(barrier, dev - 1)
    )
    for copy in loads_g:
        copy.wait()
    negate(mid.at[1])
    sandwich_and_send(r_e, mid.at[1], greater_out, greater_in, 1)
    for copy in loads_t + loads_b:
        copy.wait()
    negate(r_b)

    wait_in(lesser_in, 0)
    widen(lesser_in)
    for g in range(ROWS // group):
        spec_l[:, lanes_of(g)] = spectrum(g)
    wait_in(greater_in, 1)
    widen(greater_in)
    element_stage(True, polar_out)
    send_blocks(polar_out, polar_in, 2)

    wait_in(polar_in, 2)
    assemble(polar_in, mid.at[2])
    sandwich_and_send(r_b, mid.at[2], screen_out, screen_in, 3)

    wait_in(screen_in, 3)
    widen(screen_in)
    element_stage(False, self_out)
    send_blocks(self_out, self_in, 4)

    wait_in(self_in, 4)
    assemble(self_in, mid.at[3])
    outs = []
    for k in range(2):
        right = sandwich_half(r_e, mid.at[3], k * half)
        for part in range(2):
            result[part, k * half : (k + 1) * half, :] = right[:, part * width : (part + 1) * width]
            rows = pl.ds(k * half, half)
            copy = pltpu.make_async_copy(
                result.at[part, rows, :], out_hbm.at[0, part, rows, :], out_sem.at[2 * k + part]
            )
            copy.start()
            outs.append(copy)
    for copy in outs:
        copy.wait()
    for phase in range(5):
        view = lesser_in.at[pl.ds(0, dev - 1)]
        pltpu.make_async_copy(view, view, send_sem.at[phase]).wait()


def tables(n):
    length = 2 * n
    phase = np.arange(length)[:, None] * np.arange(n)[None, :] % length
    angle = phase * (2.0 * math.pi / length)
    cosine, sine = np.cos(angle), np.sin(angle)
    forward = np.block([[cosine, sine], [-sine, cosine]])
    return forward.astype(np.float32), forward.T.astype(np.float32)


def shards(plan, gr_electron, self_lesser, self_greater, gr_boson):
    width, dev = plan.width, plan.devices
    forward, inverse = tables(dev)
    scale = 1.0 / (2 * dev * math.sqrt(dev))
    any_spec = pl.BlockSpec(memory_space=pl.ANY)
    by_owner = pltpu.VMEM((plan.row_tiles, plan.col_tiles, 2 * ROWS, LANES), BF16)
    by_energy = pltpu.VMEM((dev, 2 * ROWS, LANES), BF16)
    return pl.pallas_call(
        functools.partial(kernel, plan, scale),
        out_shape=jax.ShapeDtypeStruct((1, 2, width, width), BF16),
        in_specs=[any_spec] * 6,
        out_specs=any_spec,
        scratch_shapes=[
            pltpu.VMEM((2 * width, 2 * width), BF16),
            pltpu.VMEM((2 * width, 2 * width), BF16),
            pltpu.VMEM((4, 2 * width, 2 * width), BF16),
            pltpu.VMEM((4 * dev, 2 * dev), BF16),
            pltpu.VMEM((2 * dev, 4 * dev), BF16),
            by_owner,
            by_owner,
            by_owner,
            by_energy,
            by_energy,
            by_energy,
            by_energy,
            by_energy,
            by_energy,
            by_energy,
            pltpu.VMEM((dev * 2 * ROWS, LANES), F32),
            pltpu.VMEM((4 * dev, ROWS * LANES), F32),
            pltpu.VMEM((2, width, width), BF16),
            pltpu.SemaphoreType.DMA((14,)),
            pltpu.SemaphoreType.DMA((5,)),
            pltpu.SemaphoreType.DMA((5,)),
            pltpu.SemaphoreType.DMA((4,)),
        ],
        compiler_params=pltpu.CompilerParams(
            collective_id=0, has_side_effects=True, vmem_limit_bytes=60 * 1024 * 1024
        ),
        name="gw_step",
    )(
        gr_electron,
        self_lesser,
        self_greater,
        gr_boson,
        jnp.asarray(forward).astype(BF16),
        jnp.asarray(inverse).astype(BF16),
    )


def solution(mesh):
    def step(gr_electron, self_lesser, self_greater, gr_boson):
        plan = Plan(mesh.shape["energy"], mesh.shape["tile"], gr_electron.shape[3])
        return shards(plan, gr_electron, self_lesser, self_greater, gr_boson)

    spec = P(("energy", "tile"), None, None, None)
    return jax.shard_map(step, mesh=mesh, in_specs=(spec,) * 4, out_specs=spec, check_vma=False)
```

```python
import functools
import math

import jax
import jax.numpy as jnp
import numpy as np
from jax import lax
from jax.experimental import pallas as pl
from jax.experimental.pallas import tpu as pltpu
from jax.sharding import PartitionSpec as P

MESH = pl.DeviceIdType.MESH
ROWS = 8
LANES = 128
BF16 = jnp.bfloat16
F32 = jnp.float32
PHASES = 4


class Plan:
    def __init__(self, n_energy, n_tile, width):
        self.n_energy, self.n_tile, self.width = n_energy, n_tile, width
        self.devices = n_energy * n_tile
        self.ny = 4 if n_energy % 4 == 0 else 2
        self.nxh = 2 if n_energy // self.ny == 8 else 1
        self.nz = n_energy // (self.ny * self.nxh)
        self.nxl = 2 if n_tile == 4 else 1
        self.nc = n_tile // self.nxl
        self.nx = self.nxh * self.nxl
        self.row_tiles = n_energy
        self.col_tiles = n_tile
        self.half = width // 2
        assert self.half == n_energy * ROWS and width == n_tile * LANES


class Partners:
    def __init__(self, plan):
        self.plan = plan
        e, t = lax.axis_index("energy"), lax.axis_index("tile")
        y = e // (plan.nxh * plan.nz)
        x = (e // plan.nz) % plan.nxh * plan.nxl + t // plan.nc
        self.z, self.c = e % plan.nz, t % plan.nc
        self.sign = 1 - 2 * self.c
        self.y_terms = [(y + plan.ny + self.sign * j) % plan.ny * (plan.nxh * plan.nz) for j in range(plan.ny)]
        xs = [(x + plan.nx + self.sign * j) % plan.nx for j in range(plan.nx)]
        self.xh_terms = [v // plan.nxl * plan.nz for v in xs]
        self.xl_terms = [v % plan.nxl * plan.nc for v in xs]

    def block(self, j, skip, act):
        plan = self.plan
        z = (self.z + plan.nz + self.sign * (j % plan.nz)) % plan.nz
        c = (self.c + j // plan.nz) % plan.nc
        for jx in range(plan.nx):
            for jy in range(plan.ny):
                if skip and jx == 0 and jy == 0:
                    continue
                act(self.y_terms[jy] + self.xh_terms[jx] + z, self.xl_terms[jx] + c)

    def each(self, act):
        self.block(0, True, act)
        if self.plan.nz * self.plan.nc > 1:

            @pl.loop(1, self.plan.nz * self.plan.nc)
            def _(j):
                self.block(j, False, act)


def kernel(
    plan,
    scale,
    gre_hbm,
    sl_hbm,
    sg_hbm,
    grb_hbm,
    fwd_hbm,
    inv_hbm,
    result,
    r_e,
    r_b,
    mid,
    fwd,
    inv,
    pair_out,
    pair_in,
    screen_out,
    screen_in,
    polar_out,
    polar_in,
    self_out,
    self_in,
    wide,
    back_wide,
    spec_l,
    left_sum,
    in_sem,
    send_sem,
    recv_sem,
):
    width, half, dev = plan.width, plan.half, plan.devices
    me_e, me_t = lax.axis_index("energy"), lax.axis_index("tile")
    me = me_e * plan.n_tile + me_t
    partners = Partners(plan)
    scope = jax.named_scope

    def load(src, dst, k):
        copy = pltpu.make_async_copy(src, dst, in_sem.at[k])
        copy.start()
        return copy

    lo, hi = pl.ds(0, width), pl.ds(width, width)

    def load_matrix(src, dst, k):
        return [
            load(src.at[0, 0], dst.at[lo, lo], k),
            load(src.at[0, 1], dst.at[lo, hi], k + 1),
            load(src.at[0, 0], dst.at[hi, hi], k + 2),
        ]

    loads_r = load_matrix(gre_hbm, r_e, 0)
    loads_l = load_matrix(sl_hbm, mid.at[0], 3)
    loads_g = load_matrix(sg_hbm, mid.at[1], 6)
    loads_t = [load(fwd_hbm, fwd, 9), load(inv_hbm, inv, 10)]
    loads_b = load_matrix(grb_hbm, r_b, 11)

    barrier = pltpu.get_barrier_semaphore()

    with scope("signal"):
        partners.each(lambda e, t: pl.semaphore_signal(barrier, inc=1, device_id=(e, t), device_id_type=MESH))

    def negate(ref):
        ref[width:, :width] = -ref[:width, width:]

    def right_product(left, outer):
        return lax.dot_general(left, outer[...], (((1,), (1,)), ((), ())), preferred_element_type=F32)

    def rows_of(h):
        return pl.ds(h * half, half)

    def sandwich_half(outer, middle, h):
        left = jnp.dot(outer[rows_of(h), :], middle[...], preferred_element_type=F32).astype(BF16)
        return right_product(left, outer)

    def left_part(outer, middle, rows, h):
        cols = (rows_of(h), pl.ds(width + h * half, half))
        return sum(jnp.dot(outer[rows, k], middle[k, :], preferred_element_type=F32) for k in cols)

    def to_blocks(right, blocks, row0):
        for ct in range(plan.col_tiles):
            pieces = [
                right[:, part * width + ct * LANES : part * width + (ct + 1) * LANES].reshape(
                    plan.row_tiles, ROWS, LANES
                )
                for part in range(2)
            ]
            blocks[:, ct, row0 : row0 + 2 * ROWS, :] = jnp.concatenate(pieces, axis=1).astype(BF16)

    def send(source, own, landing, slot):
        with scope("send"):
            partners.each(
                lambda e, t: pltpu.make_async_remote_copy(
                    src_ref=source(e, t),
                    dst_ref=landing.at[me],
                    send_sem=send_sem.at[slot],
                    recv_sem=recv_sem.at[slot],
                    device_id=(e, t),
                    device_id_type=MESH,
                ).start()
            )
        landing[me] = own

    def send_blocks(blocks, landing, slot):
        send(lambda e, t: blocks.at[e, t], blocks[me_e, me_t], landing, slot)

    def send_energies(blocks, landing, slot):
        send(lambda e, t: blocks.at[e * plan.n_tile + t], blocks[me], landing, slot)

    def wait_for(landing, sem, slot):
        view = landing.at[pl.ds(0, dev - 1)]
        pltpu.make_async_copy(view, view, sem.at[slot]).wait()

    step = 8

    def widen(landing, rows):
        @pl.loop(0, dev // step)
        def _(i):
            block = landing[pl.ds(i * step, step)].astype(F32)
            start = pl.multiple_of(i * step * rows, 8)
            wide[pl.ds(start, step * rows), :] = block.reshape(step * rows, LANES)

    group = 4
    length = 2 * dev

    def spectrum(g, first, rows):
        x = jnp.concatenate(
            [
                jnp.concatenate(
                    [
                        wide[pl.ds(first + part * ROWS + g * group + i, dev, stride=rows), :].astype(BF16)
                        for part in range(2)
                    ],
                    axis=0,
                )
                for i in range(group)
            ],
            axis=1,
        )
        return jnp.dot(fwd[...], x, preferred_element_type=F32)

    def back(g, p_re, p_im):
        p = jnp.concatenate([p_re.astype(BF16), p_im.astype(BF16)], axis=0)
        field = jnp.dot(inv[...], p, preferred_element_type=F32) * scale
        for i in range(group):
            for part in range(2):
                back_wide[pl.ds(part * ROWS + g * group + i, dev, stride=2 * ROWS), :] = field[
                    part * dev : (part + 1) * dev, i * LANES : (i + 1) * LANES
                ]

    def narrow(blocks):
        @pl.loop(0, dev // step)
        def _(i):
            start = pl.multiple_of(i * step * 2 * ROWS, 8)
            block = back_wide[pl.ds(start, step * 2 * ROWS), :].astype(BF16)
            blocks[pl.ds(i * step, step)] = block.reshape(step, 2 * ROWS, LANES)

    def lanes_of(h, g):
        start = (h * ROWS + g * group) * LANES
        return slice(start, start + group * LANES)

    def polar_half(h):
        widen(pair_in.at[h], 4 * ROWS)
        for g in range(ROWS // group):
            spec = spectrum(g, 0, 4 * ROWS)
            spec_l[:, lanes_of(h, g)] = spec
            l_re, l_im = spec[:length], spec[length:]
            spec = spectrum(g, 2 * ROWS, 4 * ROWS)
            g_re, g_im = spec[:length], spec[length:]
            back(g, l_re * g_re + l_im * g_im, l_im * g_re - l_re * g_im)
        narrow(polar_out.at[h])

    def self_half(h):
        widen(screen_in.at[h], 2 * ROWS)
        for g in range(ROWS // group):
            spec = spectrum(g, 0, 2 * ROWS)
            s_re, s_im = spec[:length], spec[length:]
            l_re, l_im = spec_l[:length, lanes_of(h, g)], spec_l[length:, lanes_of(h, g)]
            back(g, l_re * s_re - l_im * s_im, l_re * s_im + l_im * s_re)
        narrow(self_out.at[h])

    def assemble(landing, dst, h):
        rows, rows_low = rows_of(h), pl.ds(width + h * half, half)
        for ct in range(plan.col_tiles):
            tiles = jnp.concatenate(
                [landing[pl.ds(rt * plan.n_tile + ct, 1)] for rt in range(plan.row_tiles)], axis=0
            ).astype(F32)
            real = tiles[:, :ROWS, :].reshape(half, LANES).astype(BF16)
            imag = tiles[:, ROWS:, :].reshape(half, LANES).astype(BF16)
            cols, cols_im = slice(ct * LANES, (ct + 1) * LANES), slice(width + ct * LANES, width + (ct + 1) * LANES)
            dst[rows, cols] = real
            dst[rows_low, cols_im] = real
            dst[rows, cols_im] = imag
            dst[rows_low, cols] = -imag

    with scope("load"):
        for copy in loads_r + loads_l + loads_g:
            copy.wait()
        negate(r_e)
        negate(mid.at[0])
        negate(mid.at[1])
    for h in range(2):
        with scope("pair"):
            to_blocks(sandwich_half(r_e, mid.at[0], h), pair_out.at[h], 0)
            to_blocks(sandwich_half(r_e, mid.at[1], h), pair_out.at[h], 2 * ROWS)
        if h == 0:
            with scope("meet"):
                pl.semaphore_wait(barrier, dev - 1)
        send_blocks(pair_out.at[h], pair_in.at[h], h)
    with scope("load2"):
        for copy in loads_t + loads_b:
            copy.wait()
        negate(r_b)

    for h in range(2):
        with scope("wait_pair"):
            wait_for(pair_in.at[h], recv_sem, h)
        with scope("polar"):
            polar_half(h)
        send_energies(polar_out.at[h], polar_in.at[h], 2 + h)

    with scope("wait_polar"):
        wait_for(polar_in.at[0], recv_sem, 2)
    with scope("left_polar"):
        assemble(polar_in.at[0], mid.at[2], 0)
        left_sum[...] = left_part(r_b, mid.at[2], pl.ds(0, width), 0)
    with scope("wait_polar"):
        wait_for(polar_in.at[1], recv_sem, 3)
    with scope("left_polar"):
        assemble(polar_in.at[1], mid.at[2], 1)
    for h in range(2):
        with scope("screened"):
            left = (left_sum[rows_of(h), :] + left_part(r_b, mid.at[2], rows_of(h), 1)).astype(BF16)
            to_blocks(right_product(left, r_b), screen_out.at[h], 0)
        send_blocks(screen_out.at[h], screen_in.at[h], 4 + h)

    for h in range(2):
        with scope("wait_screened"):
            wait_for(screen_in.at[h], recv_sem, 4 + h)
        with scope("self_energy"):
            self_half(h)
        send_energies(self_out.at[h], self_in.at[h], 6 + h)

    with scope("wait_self"):
        wait_for(self_in.at[0], recv_sem, 6)
    with scope("left_self"):
        assemble(self_in.at[0], mid.at[3], 0)
        left_sum[...] = left_part(r_e, mid.at[3], pl.ds(0, width), 0)
    with scope("wait_self"):
        wait_for(self_in.at[1], recv_sem, 7)
    with scope("lesser_new"):
        assemble(self_in.at[1], mid.at[3], 1)
        for h in range(2):
            left = (left_sum[rows_of(h), :] + left_part(r_e, mid.at[3], rows_of(h), 1)).astype(BF16)
            right = right_product(left, r_e).astype(BF16)
            for part in range(2):
                result[0, part, h * half : (h + 1) * half, :] = right[:, part * width : (part + 1) * width]
    with scope("finish"):
        for slot in range(2 * PHASES):
            landing = (pair_in, polar_in, screen_in, self_in)[slot // 2]
            wait_for(landing.at[slot % 2], send_sem, slot)


def tables(n):
    length = 2 * n
    phase = np.arange(length)[:, None] * np.arange(n)[None, :] % length
    angle = phase * (2.0 * math.pi / length)
    cosine, sine = np.cos(angle), np.sin(angle)
    forward = np.block([[cosine, sine], [-sine, cosine]])
    return forward.astype(np.float32), forward.T.astype(np.float32)


def shards(plan, gr_electron, self_lesser, self_greater, gr_boson):
    width, dev = plan.width, plan.devices
    forward, inverse = tables(dev)
    scale = 1.0 / (2 * dev * math.sqrt(dev))
    any_spec = pl.BlockSpec(memory_space=pl.ANY)

    def by_owner(rows):
        return pltpu.VMEM((2, plan.row_tiles, plan.col_tiles, rows, LANES), BF16)

    def by_energy(rows):
        return pltpu.VMEM((2, dev, rows, LANES), BF16)

    return pl.pallas_call(
        functools.partial(kernel, plan, scale),
        out_shape=pltpu.VMEM((1, 2, width, width), BF16),
        in_specs=[any_spec] * 6,
        out_specs=pl.BlockSpec(memory_space=pltpu.VMEM),
        scratch_shapes=[
            pltpu.VMEM((2 * width, 2 * width), BF16),
            pltpu.VMEM((2 * width, 2 * width), BF16),
            pltpu.VMEM((4, 2 * width, 2 * width), BF16),
            pltpu.VMEM((4 * dev, 2 * dev), BF16),
            pltpu.VMEM((2 * dev, 4 * dev), BF16),
            by_owner(4 * ROWS),
            by_energy(4 * ROWS),
            by_owner(2 * ROWS),
            by_energy(2 * ROWS),
            by_energy(2 * ROWS),
            by_energy(2 * ROWS),
            by_energy(2 * ROWS),
            by_energy(2 * ROWS),
            pltpu.VMEM((dev * 4 * ROWS, LANES), F32),
            pltpu.VMEM((dev * 2 * ROWS, LANES), F32),
            pltpu.VMEM((4 * dev, 2 * ROWS * LANES), F32),
            pltpu.VMEM((width, 2 * width), F32),
            pltpu.SemaphoreType.DMA((14,)),
            pltpu.SemaphoreType.DMA((2 * PHASES,)),
            pltpu.SemaphoreType.DMA((2 * PHASES,)),
        ],
        compiler_params=pltpu.CompilerParams(
            collective_id=0, has_side_effects=True, vmem_limit_bytes=56 * 1024 * 1024
        ),
        name="gw_step",
    )(
        gr_electron,
        self_lesser,
        self_greater,
        gr_boson,
        jnp.asarray(forward).astype(BF16),
        jnp.asarray(inverse).astype(BF16),
    )


def solution(mesh):
    def step(gr_electron, self_lesser, self_greater, gr_boson):
        plan = Plan(mesh.shape["energy"], mesh.shape["tile"], gr_electron.shape[3])
        return shards(plan, gr_electron, self_lesser, self_greater, gr_boson)

    spec = P(("energy", "tile"), None, None, None)
    return jax.shard_map(step, mesh=mesh, in_specs=(spec,) * 4, out_specs=spec, check_vma=False)
```

```python
import functools
import itertools
import math

import jax
import jax.numpy as jnp
import numpy as np
from jax import lax
from jax.experimental import pallas as pl
from jax.experimental.pallas import tpu as pltpu
from jax.sharding import PartitionSpec as P

MESH = pl.DeviceIdType.MESH
ROWS = 8
LANES = 128
BF16 = jnp.bfloat16
F32 = jnp.float32
PHASES = 4


class Plan:
    def __init__(self, n_energy, n_tile, width):
        self.n_energy, self.n_tile, self.width = n_energy, n_tile, width
        self.devices = n_energy * n_tile
        self.ny = 4 if n_energy % 4 == 0 else 2
        self.nxh = 2 if n_energy // self.ny == 8 else 1
        self.nz = n_energy // (self.ny * self.nxh)
        self.nxl = 2 if n_tile == 4 else 1
        self.nc = n_tile // self.nxl
        self.nx = self.nxh * self.nxl
        self.row_tiles = n_energy
        self.col_tiles = n_tile
        self.half = width // 2
        assert self.half == n_energy * ROWS and width == n_tile * LANES


class Partners:
    def __init__(self, plan):
        self.plan = plan
        e, t = lax.axis_index("energy"), lax.axis_index("tile")
        y = e // (plan.nxh * plan.nz)
        x = (e // plan.nz) % plan.nxh * plan.nxl + t // plan.nc
        z, c = e % plan.nz, t % plan.nc
        sign = 1 - 2 * c
        self.y_terms = [(y + plan.ny + sign * j) % plan.ny * (plan.nxh * plan.nz) for j in range(plan.ny)]
        xs = [(x + plan.nx + sign * j) % plan.nx for j in range(plan.nx)]
        self.xh_terms = [v // plan.nxl * plan.nz for v in xs]
        self.xl_terms = [v % plan.nxl * plan.nc for v in xs]
        self.c_terms = [(c + j) % plan.nc for j in range(plan.nc)]
        self.z_terms = [(z + plan.nz + sign * j) % plan.nz for j in range(plan.nz)]

        def hops(j, n):
            return min(j, n - j)

        sizes = (plan.nc, plan.nz, plan.nx, plan.ny)
        others = list(itertools.product(*map(range, sizes)))[1:]
        self.order = sorted(others, key=lambda p: (-sum(map(hops, p[1:], sizes[1:])), -p[0]))

    def each(self, act):
        for jc, jz, jx, jy in self.order:
            act(self.y_terms[jy] + self.xh_terms[jx] + self.z_terms[jz], self.xl_terms[jx] + self.c_terms[jc])


def kernel(
    plan,
    scale,
    gre_hbm,
    sl_hbm,
    sg_hbm,
    grb_hbm,
    fwd_hbm,
    inv_hbm,
    result,
    r_e,
    r_b,
    mid,
    fwd,
    inv,
    pair_out,
    pair_in,
    screen_out,
    screen_in,
    polar_out,
    polar_in,
    self_out,
    self_in,
    wide,
    back_wide,
    spec_l,
    left_sum,
    in_sem,
    send_sem,
    recv_sem,
):
    width, half, dev = plan.width, plan.half, plan.devices
    me_e, me_t = lax.axis_index("energy"), lax.axis_index("tile")
    me = me_e * plan.n_tile + me_t
    partners = Partners(plan)
    scope = jax.named_scope

    def load(src, dst, k):
        copy = pltpu.make_async_copy(src, dst, in_sem.at[k])
        copy.start()
        return copy

    lo, hi = pl.ds(0, width), pl.ds(width, width)

    def load_matrix(src, dst, k):
        return [load(src.at[0, 0], dst.at[lo, lo], k), load(src.at[0, 1], dst.at[lo, hi], k + 1)]

    loads_r = load_matrix(gre_hbm, r_e, 0)
    loads_l = load_matrix(sl_hbm, mid.at[0], 2)
    loads_g = load_matrix(sg_hbm, mid.at[1], 4)

    barrier = pltpu.get_barrier_semaphore()

    with scope("signal"):
        partners.each(lambda e, t: pl.semaphore_signal(barrier, inc=1, device_id=(e, t), device_id_type=MESH))

    def complete(ref):
        ref[width:, :width] = -ref[:width, width:]
        ref[width:, width:] = ref[:width, :width]

    def right_product(left, outer):
        return lax.dot_general(left, outer[...], (((1,), (1,)), ((), ())), preferred_element_type=F32)

    def rows_of(h):
        return pl.ds(h * half, half)

    def sandwich_half(outer, middle, h):
        left = jnp.dot(outer[rows_of(h), :], middle[...], preferred_element_type=F32).astype(BF16)
        return right_product(left, outer)

    def left_part(outer, middle, rows, h):
        cols = (rows_of(h), pl.ds(width + h * half, half))
        return sum(jnp.dot(outer[rows, k], middle[k, :], preferred_element_type=F32) for k in cols)

    def to_blocks(right, blocks, row0):
        for ct in range(plan.col_tiles):
            pieces = [
                right[:, part * width + ct * LANES : part * width + (ct + 1) * LANES].reshape(
                    plan.row_tiles, ROWS, LANES
                )
                for part in range(2)
            ]
            blocks[:, ct, row0 : row0 + 2 * ROWS, :] = jnp.concatenate(pieces, axis=1).astype(BF16)

    def landings(slot):
        return (pair_in, polar_in, screen_in, self_in)[slot // 2].at[slot % 2]

    def send(source, own, landing, slot):
        if slot > 0:
            with scope("gate"):
                wait_for(landings(slot - 1), send_sem, slot - 1)
        with scope("send"):
            partners.each(
                lambda e, t: pltpu.make_async_remote_copy(
                    src_ref=source(e, t),
                    dst_ref=landing.at[me],
                    send_sem=send_sem.at[slot],
                    recv_sem=recv_sem.at[slot],
                    device_id=(e, t),
                    device_id_type=MESH,
                ).start()
            )
        landing[me] = own

    def send_blocks(blocks, landing, slot):
        send(lambda e, t: blocks.at[e, t], blocks[me_e, me_t], landing, slot)

    def send_energies(blocks, landing, slot):
        send(lambda e, t: blocks.at[e * plan.n_tile + t], blocks[me], landing, slot)

    def wait_for(landing, sem, slot):
        view = landing.at[pl.ds(0, dev - 1)]
        pltpu.make_async_copy(view, view, sem.at[slot]).wait()

    step = min(16, dev)
    length = 2 * dev
    pair_pitch, field_pitch = 4 * ROWS + 8, 2 * ROWS + 8

    def widen(landing, rows, pitch):
        @pl.loop(0, dev // step)
        def _(i):
            for k in range(step):
                start = pl.multiple_of((i * step + k) * pitch, 8)
                wide[pl.ds(start, rows), :] = landing[i * step + k].astype(F32)

    def spectrum(first, pitch):
        x = jnp.concatenate(
            [
                jnp.concatenate(
                    [
                        wide[pl.ds(first + part * ROWS + i, dev, stride=pitch), :].astype(BF16)
                        for part in range(2)
                    ],
                    axis=0,
                )
                for i in range(ROWS)
            ],
            axis=1,
        )
        spec = jnp.dot(fwd[...], x, preferred_element_type=F32)
        return spec[:length], spec[length:]

    def back(p_re, p_im, blocks):
        p = jnp.concatenate([p_re.astype(BF16), p_im.astype(BF16)], axis=0)
        field = jnp.dot(inv[...], p, preferred_element_type=F32) * scale
        for i in range(ROWS):
            for part in range(2):
                back_wide[pl.ds(part * ROWS + i, dev, stride=field_pitch), :] = field[
                    part * dev : (part + 1) * dev, i * LANES : (i + 1) * LANES
                ]

        @pl.loop(0, dev // step)
        def _(i):
            for k in range(step):
                start = pl.multiple_of((i * step + k) * field_pitch, 8)
                blocks[i * step + k] = back_wide[pl.ds(start, 2 * ROWS), :].astype(BF16)

    def lanes_of(h):
        return slice(h * ROWS * LANES, (h + 1) * ROWS * LANES)

    def polar_half(h):
        widen(pair_in.at[h], 4 * ROWS, pair_pitch)
        l_re, l_im = spectrum(0, pair_pitch)
        spec_l[:length, lanes_of(h)] = l_re
        spec_l[length:, lanes_of(h)] = l_im
        g_re, g_im = spectrum(2 * ROWS, pair_pitch)
        back(l_re * g_re + l_im * g_im, l_im * g_re - l_re * g_im, polar_out.at[h])

    def self_half(h):
        widen(screen_in.at[h], 2 * ROWS, field_pitch)
        s_re, s_im = spectrum(0, field_pitch)
        l_re, l_im = spec_l[:length, lanes_of(h)], spec_l[length:, lanes_of(h)]
        back(l_re * s_re - l_im * s_im, l_re * s_im + l_im * s_re, self_out.at[h])

    def assemble(landing, dst, h, lower):
        rows, rows_low = rows_of(h), pl.ds(width + h * half, half)
        for ct in range(plan.col_tiles):
            tiles = jnp.concatenate(
                [landing[pl.ds(rt * plan.n_tile + ct, 1)] for rt in range(plan.row_tiles)], axis=0
            ).astype(F32)
            real = tiles[:, :ROWS, :].reshape(half, LANES).astype(BF16)
            imag = tiles[:, ROWS:, :].reshape(half, LANES).astype(BF16)
            cols, cols_im = slice(ct * LANES, (ct + 1) * LANES), slice(width + ct * LANES, width + (ct + 1) * LANES)
            dst[rows, cols] = real
            dst[rows, cols_im] = imag
            if lower:
                dst[rows_low, cols_im] = real
                dst[rows_low, cols] = -imag

    with scope("load"):
        for copy in loads_r + loads_l:
            copy.wait()
        complete(r_e)
        complete(mid.at[0])
    later = []
    for h in range(2):
        with scope("pair"):
            to_blocks(sandwich_half(r_e, mid.at[0], h), pair_out.at[h], 0)
            if h == 0:
                for copy in loads_g:
                    copy.wait()
                complete(mid.at[1])
            to_blocks(sandwich_half(r_e, mid.at[1], h), pair_out.at[h], 2 * ROWS)
        if h == 0:
            with scope("meet"):
                pl.semaphore_wait(barrier, dev - 1)
        send_blocks(pair_out.at[h], pair_in.at[h], h)
        if h == 0:
            later = [load(fwd_hbm, fwd, 6), load(inv_hbm, inv, 7)] + load_matrix(grb_hbm, r_b, 8)
    with scope("load2"):
        for copy in later:
            copy.wait()
        complete(r_b)

    for h in range(2):
        with scope("wait_pair"):
            wait_for(pair_in.at[h], recv_sem, h)
        with scope("polar"):
            polar_half(h)
        send_energies(polar_out.at[h], polar_in.at[h], 2 + h)

    with scope("wait_polar"):
        wait_for(polar_in.at[0], recv_sem, 2)
    with scope("left_polar"):
        assemble(polar_in.at[0], mid.at[2], 0, True)
        left_sum[...] = left_part(r_b, mid.at[2], pl.ds(0, width), 0)
    with scope("wait_polar"):
        wait_for(polar_in.at[1], recv_sem, 3)
    with scope("left_polar"):
        assemble(polar_in.at[1], mid.at[2], 1, True)
    for h in range(2):
        with scope("screened"):
            left = (left_sum[rows_of(h), :] + left_part(r_b, mid.at[2], rows_of(h), 1)).astype(BF16)
            to_blocks(right_product(left, r_b), screen_out.at[h], 0)
        send_blocks(screen_out.at[h], screen_in.at[h], 4 + h)

    for h in range(2):
        with scope("wait_screened"):
            wait_for(screen_in.at[h], recv_sem, 4 + h)
        with scope("self_energy"):
            self_half(h)
        send_energies(self_out.at[h], self_in.at[h], 6 + h)

    def right_first(h):
        assemble(self_in.at[h], mid.at[0], h, False)
        right = right_product(mid[0, rows_of(h), :], r_e).astype(BF16)
        mid[1, rows_of(h), :] = right
        low = pl.ds(width + h * half, half)
        mid[1, low, :width] = -right[:, width:]
        mid[1, low, width:] = right[:, :width]
        return left_part(r_e, mid.at[1], pl.ds(0, width), h)

    with scope("wait_self"):
        wait_for(self_in.at[0], recv_sem, 6)
    with scope("right_self"):
        left_sum[...] = right_first(0)
    with scope("wait_self"):
        wait_for(self_in.at[1], recv_sem, 7)
    with scope("lesser_new"):
        total = (left_sum[...] + right_first(1)).astype(BF16)
        for part in range(2):
            result[0, part] = total[:, part * width : (part + 1) * width]
    with scope("finish"):
        wait_for(landings(2 * PHASES - 1), send_sem, 2 * PHASES - 1)


def tables(n):
    length = 2 * n
    phase = np.arange(length)[:, None] * np.arange(n)[None, :] % length
    angle = phase * (2.0 * math.pi / length)
    cosine, sine = np.cos(angle), np.sin(angle)
    forward = np.block([[cosine, sine], [-sine, cosine]])
    return forward.astype(np.float32), forward.T.astype(np.float32)


def shards(plan, gr_electron, self_lesser, self_greater, gr_boson):
    width, dev = plan.width, plan.devices
    forward, inverse = tables(dev)
    scale = 1.0 / (2 * dev * math.sqrt(dev))
    any_spec = pl.BlockSpec(memory_space=pl.ANY)

    def by_owner(rows):
        return pltpu.VMEM((2, plan.row_tiles, plan.col_tiles, rows, LANES), BF16)

    def by_energy(rows):
        return pltpu.VMEM((2, dev, rows, LANES), BF16)

    return pl.pallas_call(
        functools.partial(kernel, plan, scale),
        out_shape=pltpu.VMEM((1, 2, width, width), BF16),
        in_specs=[any_spec] * 6,
        out_specs=pl.BlockSpec(memory_space=pltpu.VMEM),
        scratch_shapes=[
            pltpu.VMEM((2 * width, 2 * width), BF16),
            pltpu.VMEM((2 * width, 2 * width), BF16),
            pltpu.VMEM((3, 2 * width, 2 * width), BF16),
            pltpu.VMEM((4 * dev, 2 * dev), BF16),
            pltpu.VMEM((2 * dev, 4 * dev), BF16),
            by_owner(4 * ROWS),
            by_energy(4 * ROWS),
            by_owner(2 * ROWS),
            by_energy(2 * ROWS),
            by_energy(2 * ROWS),
            by_energy(2 * ROWS),
            by_energy(2 * ROWS),
            by_energy(2 * ROWS),
            pltpu.VMEM((dev * (4 * ROWS + 8), LANES), F32),
            pltpu.VMEM((dev * (2 * ROWS + 8), LANES), F32),
            pltpu.VMEM((4 * dev, 2 * ROWS * LANES), F32),
            pltpu.VMEM((width, 2 * width), F32),
            pltpu.SemaphoreType.DMA((10,)),
            pltpu.SemaphoreType.DMA((2 * PHASES,)),
            pltpu.SemaphoreType.DMA((2 * PHASES,)),
        ],
        compiler_params=pltpu.CompilerParams(
            collective_id=0, has_side_effects=True, vmem_limit_bytes=56 * 1024 * 1024
        ),
        name="gw_step",
    )(
        gr_electron,
        self_lesser,
        self_greater,
        gr_boson,
        jnp.asarray(forward).astype(BF16),
        jnp.asarray(inverse).astype(BF16),
    )


def solution(mesh):
    def step(gr_electron, self_lesser, self_greater, gr_boson):
        plan = Plan(mesh.shape["energy"], mesh.shape["tile"], gr_electron.shape[3])
        return shards(plan, gr_electron, self_lesser, self_greater, gr_boson)

    spec = P(("energy", "tile"), None, None, None)
    return jax.shard_map(step, mesh=mesh, in_specs=(spec,) * 4, out_specs=spec, check_vma=False)
```

```python
import functools
import itertools
import math

import jax
import jax.numpy as jnp
import numpy as np
from jax import lax
from jax.experimental import pallas as pl
from jax.experimental.pallas import tpu as pltpu
from jax.sharding import PartitionSpec as P

MESH = pl.DeviceIdType.MESH
ROWS = 8
LANES = 128
BF16 = jnp.bfloat16
F32 = jnp.float32
PHASES = 4


class Plan:
    def __init__(self, n_energy, n_tile, width):
        self.n_energy, self.n_tile, self.width = n_energy, n_tile, width
        self.devices = n_energy * n_tile
        self.ny = 4 if n_energy % 4 == 0 else 2
        self.nxh = 2 if n_energy // self.ny == 8 else 1
        self.nz = n_energy // (self.ny * self.nxh)
        self.nxl = 2 if n_tile == 4 else 1
        self.nc = n_tile // self.nxl
        self.nx = self.nxh * self.nxl
        self.row_tiles = n_energy
        self.col_tiles = n_tile
        self.half = width // 2
        assert self.half == n_energy * ROWS and width == n_tile * LANES


class Partners:
    def __init__(self, plan):
        self.plan = plan
        e, t = lax.axis_index("energy"), lax.axis_index("tile")
        y = e // (plan.nxh * plan.nz)
        x = (e // plan.nz) % plan.nxh * plan.nxl + t // plan.nc
        z, c = e % plan.nz, t % plan.nc
        sign = 1 - 2 * c
        self.y_terms = [(y + plan.ny + sign * j) % plan.ny * (plan.nxh * plan.nz) for j in range(plan.ny)]
        xs = [(x + plan.nx + sign * j) % plan.nx for j in range(plan.nx)]
        self.xh_terms = [v // plan.nxl * plan.nz for v in xs]
        self.xl_terms = [v % plan.nxl * plan.nc for v in xs]
        self.c_terms = [(c + j) % plan.nc for j in range(plan.nc)]
        self.z_terms = [(z + plan.nz + sign * j) % plan.nz for j in range(plan.nz)]

        def hops(j, n):
            return min(j, n - j)

        sizes = (plan.nc, plan.nz, plan.nx, plan.ny)
        others = list(itertools.product(*map(range, sizes)))[1:]
        self.order = sorted(others, key=lambda p: (-sum(map(hops, p[1:], sizes[1:])), -p[0]))

    def each_by_core(self, act):
        plan = self.plan
        chips = [p[1:] for p in self.order if p[0] == 0]
        for core in range(plan.nc):
            for jz, jx, jy in chips:
                act(self.y_terms[jy] + self.xh_terms[jx] + self.z_terms[jz], self.xl_terms[jx] + core)
            if core == 0 and plan.nc > 1:
                act(self.y_terms[0] + self.xh_terms[0] + self.z_terms[0], self.xl_terms[0] + self.c_terms[1])

    def each(self, act):
        for jc, jz, jx, jy in self.order:
            act(self.y_terms[jy] + self.xh_terms[jx] + self.z_terms[jz], self.xl_terms[jx] + self.c_terms[jc])


def kernel(
    plan,
    scale,
    gre_hbm,
    sl_hbm,
    sg_hbm,
    grb_hbm,
    fwd_hbm,
    inv_hbm,
    result,
    r_e,
    r_b,
    mid,
    fwd,
    inv,
    pair_out,
    pair_in,
    screen_out,
    screen_in,
    polar_out,
    polar_in,
    self_out,
    self_in,
    wide,
    back_wide,
    spec_l,
    left_sum,
    in_sem,
    send_sem,
    recv_sem,
):
    width, half, dev = plan.width, plan.half, plan.devices
    me_e, me_t = lax.axis_index("energy"), lax.axis_index("tile")
    me = me_e * plan.n_tile + me_t
    partners = Partners(plan)
    scope = jax.named_scope

    def load(src, dst, k):
        copy = pltpu.make_async_copy(src, dst, in_sem.at[k])
        copy.start()
        return copy

    lo, hi = pl.ds(0, width), pl.ds(width, width)

    def load_matrix(src, dst, k):
        return [load(src.at[0, 0], dst.at[lo, lo], k), load(src.at[0, 1], dst.at[lo, hi], k + 1)]

    loads_r = load_matrix(gre_hbm, r_e, 0)
    loads_l = load_matrix(sl_hbm, mid.at[0], 2)
    loads_g = load_matrix(sg_hbm, mid.at[1], 4)

    barrier = pltpu.get_barrier_semaphore()

    with scope("signal"):
        partners.each(lambda e, t: pl.semaphore_signal(barrier, inc=1, device_id=(e, t), device_id_type=MESH))

    def complete(ref):
        ref[width:, :width] = -ref[:width, width:]
        ref[width:, width:] = ref[:width, :width]

    def right_product(left, outer):
        return lax.dot_general(left, outer[...], (((1,), (1,)), ((), ())), preferred_element_type=F32)

    def rows_of(h):
        return pl.ds(h * half, half)

    def sandwich_half(outer, middle, h):
        left = jnp.dot(outer[rows_of(h), :], middle[...], preferred_element_type=F32).astype(BF16)
        return right_product(left, outer)

    def left_part(outer, middle, rows, h):
        cols = (rows_of(h), pl.ds(width + h * half, half))
        return sum(jnp.dot(outer[rows, k], middle[k, :], preferred_element_type=F32) for k in cols)

    def to_blocks(right, blocks, row0):
        for ct in range(plan.col_tiles):
            pieces = [
                right[:, part * width + ct * LANES : part * width + (ct + 1) * LANES].reshape(
                    plan.row_tiles, ROWS, LANES
                )
                for part in range(2)
            ]
            blocks[:, ct, row0 : row0 + 2 * ROWS, :] = jnp.concatenate(pieces, axis=1).astype(BF16)

    def landings(slot):
        return (pair_in, polar_in, screen_in, self_in)[slot // 2].at[slot % 2]

    def send(source, own, landing, slot, walk=None):
        @pl.when(me >= 0)
        def _():
            if slot > 0:
                with scope("gate"):
                    wait_for(landings(slot - 1), send_sem, slot - 1)
            with scope("send"):
                (walk or partners.each)(
                    lambda e, t: pltpu.make_async_remote_copy(
                        src_ref=source(e, t),
                        dst_ref=landing.at[me],
                        send_sem=send_sem.at[slot],
                        recv_sem=recv_sem.at[slot],
                        device_id=(e, t),
                        device_id_type=MESH,
                    ).start()
                )

        landing[me] = own

    def send_blocks(blocks, landing, slot):
        send(lambda e, t: blocks.at[e, t], blocks[me_e, me_t], landing, slot)

    def send_energies(blocks, landing, slot, walk=None):
        send(lambda e, t: blocks.at[e * plan.n_tile + t], blocks[me], landing, slot, walk)

    def wait_for(landing, sem, slot):
        view = landing.at[pl.ds(0, dev - 1)]
        pltpu.make_async_copy(view, view, sem.at[slot]).wait()

    step = min(16, dev)
    length = 2 * dev
    pair_pitch, field_pitch = 4 * ROWS + 8, 2 * ROWS + 8

    def widen(landing, rows, pitch):
        @pl.loop(0, dev // step)
        def _(i):
            for k in range(step):
                start = pl.multiple_of((i * step + k) * pitch, 8)
                wide[pl.ds(start, rows), :] = landing[i * step + k].astype(F32)

    def spectrum(first, pitch):
        x = jnp.concatenate(
            [
                jnp.concatenate(
                    [
                        wide[pl.ds(first + part * ROWS + i, dev, stride=pitch), :].astype(BF16)
                        for part in range(2)
                    ],
                    axis=0,
                )
                for i in range(ROWS)
            ],
            axis=1,
        )
        spec = jnp.dot(fwd[...], x, preferred_element_type=F32)
        return spec[:length], spec[length:]

    def back(p_re, p_im, blocks):
        p = jnp.concatenate([p_re.astype(BF16), p_im.astype(BF16)], axis=0)
        field = jnp.dot(inv[...], p, preferred_element_type=F32) * scale
        for i in range(ROWS):
            for part in range(2):
                back_wide[pl.ds(part * ROWS + i, dev, stride=field_pitch), :] = field[
                    part * dev : (part + 1) * dev, i * LANES : (i + 1) * LANES
                ]

        @pl.loop(0, dev // step)
        def _(i):
            for k in range(step):
                start = pl.multiple_of((i * step + k) * field_pitch, 8)
                blocks[i * step + k] = back_wide[pl.ds(start, 2 * ROWS), :].astype(BF16)

    def lanes_of(h):
        return slice(h * ROWS * LANES, (h + 1) * ROWS * LANES)

    def polar_half(h):
        widen(pair_in.at[h], 4 * ROWS, pair_pitch)
        l_re, l_im = spectrum(0, pair_pitch)
        spec_l[:length, lanes_of(h)] = l_re
        spec_l[length:, lanes_of(h)] = l_im
        g_re, g_im = spectrum(2 * ROWS, pair_pitch)
        back(l_re * g_re + l_im * g_im, l_im * g_re - l_re * g_im, polar_out.at[h])

    def self_half(h):
        widen(screen_in.at[h], 2 * ROWS, field_pitch)
        s_re, s_im = spectrum(0, field_pitch)
        l_re, l_im = spec_l[:length, lanes_of(h)], spec_l[length:, lanes_of(h)]
        back(l_re * s_re - l_im * s_im, l_re * s_im + l_im * s_re, self_out.at[h])

    def assemble(landing, dst, h, lower):
        rows, rows_low = rows_of(h), pl.ds(width + h * half, half)
        for ct in range(plan.col_tiles):
            tiles = jnp.concatenate(
                [landing[pl.ds(rt * plan.n_tile + ct, 1)] for rt in range(plan.row_tiles)], axis=0
            ).astype(F32)
            real = tiles[:, :ROWS, :].reshape(half, LANES).astype(BF16)
            imag = tiles[:, ROWS:, :].reshape(half, LANES).astype(BF16)
            cols, cols_im = slice(ct * LANES, (ct + 1) * LANES), slice(width + ct * LANES, width + (ct + 1) * LANES)
            dst[rows, cols] = real
            dst[rows, cols_im] = imag
            if lower:
                dst[rows_low, cols_im] = real
                dst[rows_low, cols] = -imag

    with scope("load"):
        for copy in loads_r + loads_l:
            copy.wait()
        complete(r_e)
        complete(mid.at[0])
    later = []
    for h in range(2):
        with scope("pair"):
            to_blocks(sandwich_half(r_e, mid.at[0], h), pair_out.at[h], 0)
            if h == 0:
                for copy in loads_g:
                    copy.wait()
                complete(mid.at[1])
            to_blocks(sandwich_half(r_e, mid.at[1], h), pair_out.at[h], 2 * ROWS)
        if h == 0:
            with scope("meet"):
                pl.semaphore_wait(barrier, dev - 1)
        send_blocks(pair_out.at[h], pair_in.at[h], h)
        if h == 0:
            later = [load(fwd_hbm, fwd, 6), load(inv_hbm, inv, 7)] + load_matrix(grb_hbm, r_b, 8)
    with scope("load2"):
        for copy in later:
            copy.wait()
        complete(r_b)

    for h in range(2):
        with scope("wait_pair"):
            wait_for(pair_in.at[h], recv_sem, h)
        with scope("polar"):
            polar_half(h)
        send_energies(polar_out.at[h], polar_in.at[h], 2 + h, partners.each_by_core)

    with scope("wait_polar"):
        wait_for(polar_in.at[0], recv_sem, 2)
    with scope("left_polar"):
        assemble(polar_in.at[0], mid.at[2], 0, True)
        left_sum[...] = left_part(r_b, mid.at[2], pl.ds(0, width), 0)
    with scope("wait_polar"):
        wait_for(polar_in.at[1], recv_sem, 3)
    with scope("left_polar"):
        assemble(polar_in.at[1], mid.at[2], 1, True)
    for h in range(2):
        with scope("screened"):
            left = (left_sum[rows_of(h), :] + left_part(r_b, mid.at[2], rows_of(h), 1)).astype(BF16)
            to_blocks(right_product(left, r_b), screen_out.at[h], 0)
        send_blocks(screen_out.at[h], screen_in.at[h], 4 + h)

    for h in range(2):
        with scope("wait_screened"):
            wait_for(screen_in.at[h], recv_sem, 4 + h)
        with scope("self_energy"):
            self_half(h)
        send_energies(self_out.at[h], self_in.at[h], 6 + h)

    def right_first(h):
        assemble(self_in.at[h], mid.at[0], h, False)
        right = right_product(mid[0, rows_of(h), :], r_e).astype(BF16)
        mid[1, rows_of(h), :] = right
        low = pl.ds(width + h * half, half)
        mid[1, low, :width] = -right[:, width:]
        mid[1, low, width:] = right[:, :width]
        return left_part(r_e, mid.at[1], pl.ds(0, width), h)

    with scope("wait_self"):
        wait_for(self_in.at[0], recv_sem, 6)
    with scope("right_self"):
        left_sum[...] = right_first(0)
    with scope("wait_self"):
        wait_for(self_in.at[1], recv_sem, 7)
    with scope("lesser_new"):
        total = (left_sum[...] + right_first(1)).astype(BF16)
        for part in range(2):
            result[0, part] = total[:, part * width : (part + 1) * width]
    with scope("finish"):
        wait_for(landings(2 * PHASES - 1), send_sem, 2 * PHASES - 1)


def tables(n):
    length = 2 * n
    phase = np.arange(length)[:, None] * np.arange(n)[None, :] % length
    angle = phase * (2.0 * math.pi / length)
    cosine, sine = np.cos(angle), np.sin(angle)
    forward = np.block([[cosine, sine], [-sine, cosine]])
    return forward.astype(np.float32), forward.T.astype(np.float32)


def shards(plan, gr_electron, self_lesser, self_greater, gr_boson):
    width, dev = plan.width, plan.devices
    forward, inverse = tables(dev)
    scale = 1.0 / (2 * dev * math.sqrt(dev))
    any_spec = pl.BlockSpec(memory_space=pl.ANY)

    def by_owner(rows):
        return pltpu.VMEM((2, plan.row_tiles, plan.col_tiles, rows, LANES), BF16)

    def by_energy(rows):
        return pltpu.VMEM((2, dev, rows, LANES), BF16)

    return pl.pallas_call(
        functools.partial(kernel, plan, scale),
        out_shape=pltpu.VMEM((1, 2, width, width), BF16),
        in_specs=[any_spec] * 6,
        out_specs=pl.BlockSpec(memory_space=pltpu.VMEM),
        scratch_shapes=[
            pltpu.VMEM((2 * width, 2 * width), BF16),
            pltpu.VMEM((2 * width, 2 * width), BF16),
            pltpu.VMEM((3, 2 * width, 2 * width), BF16),
            pltpu.VMEM((4 * dev, 2 * dev), BF16),
            pltpu.VMEM((2 * dev, 4 * dev), BF16),
            by_owner(4 * ROWS),
            by_energy(4 * ROWS),
            by_owner(2 * ROWS),
            by_energy(2 * ROWS),
            by_energy(2 * ROWS),
            by_energy(2 * ROWS),
            by_energy(2 * ROWS),
            by_energy(2 * ROWS),
            pltpu.VMEM((dev * (4 * ROWS + 8), LANES), F32),
            pltpu.VMEM((dev * (2 * ROWS + 8), LANES), F32),
            pltpu.VMEM((4 * dev, 2 * ROWS * LANES), F32),
            pltpu.VMEM((width, 2 * width), F32),
            pltpu.SemaphoreType.DMA((10,)),
            pltpu.SemaphoreType.DMA((2 * PHASES,)),
            pltpu.SemaphoreType.DMA((2 * PHASES,)),
        ],
        compiler_params=pltpu.CompilerParams(
            collective_id=0, has_side_effects=True, vmem_limit_bytes=56 * 1024 * 1024
        ),
        name="gw_step",
    )(
        gr_electron,
        self_lesser,
        self_greater,
        gr_boson,
        jnp.asarray(forward).astype(BF16),
        jnp.asarray(inverse).astype(BF16),
    )


def solution(mesh):
    def step(gr_electron, self_lesser, self_greater, gr_boson):
        plan = Plan(mesh.shape["energy"], mesh.shape["tile"], gr_electron.shape[3])
        return shards(plan, gr_electron, self_lesser, self_greater, gr_boson)

    spec = P(("energy", "tile"), None, None, None)
    return jax.shard_map(step, mesh=mesh, in_specs=(spec,) * 4, out_specs=spec, check_vma=False)
```
